32 devices in a mesh: groups: 2 (over y), req: 8 (over z, core), head: 2 (over x), rep: 1.
Axes of the slice: x: 2, y: 2, z: 4, core: 2. Of those that a mesh axis runs over, the one named last changes fastest.
Arguments:
- candidates: bfloat16 [32768, 1024], P(('groups', 'req', 'rep')), parts along dimension 0, may hold values from -6 to 6
- candidate_request: int32 [16, 2048], P(('groups', 'req'), 'rep'), parts along dimension 0, may hold values from 0 to 7, never falling along the last dimension, each value on 1 to 512 neighbouring positions
- request_owner: int32 [128, 1], P(('groups', 'req')), parts along dimension 0, may hold values from 0 to 7; in each aligned block of 8 rows (0 to 7, 8 to 15, ...) no two rows name the same one
- request_user: int32 [128], P(('groups', 'req')), parts along dimension 0, may hold values from 0 to 7
- request_blocks: int32 [16, 8], P(('groups', 'req')), parts along dimension 0, may hold values from 1 to 4, 24 in all within a row
- kv_cache: bfloat16 [128, 512, 2048], P(('groups', 'req'), None, 'head'), parts along dimension 0, may hold values from -6 to 6
- w_in: bfloat16 [1024, 4096], P(None, 'head'), may hold values from -0.1875 to 0.1875
- w_out: bfloat16 [1024, 1024], P('head'), may hold values from -0.1875 to 0.1875
Outputs:
- ranked: bfloat16 [32768, 1024], P(('groups', 'req', 'rep'), 'head'), parts along dimension 0
The draws below stay inside these ranges and needn't reach their ends.
There are 2 independent parts, one for each index of `groups`. The reference program is written for one: setup_inputs(seed, part) draws one part's arguments, and reference() takes and returns one part's arrays. A program takes and returns all parts, laid end to end along the dimension named above; an argument that names none is the same for every part. Nothing has to cross between parts.
Inputs may be any that keep to these rules, and one draw needn't show every extreme that they name: `request_owner`: among the 8 requests of one req index at most 1 name the same owner, a bound that some block reaches of them. `request_blocks`: the 8 lengths of one req index sum to 24; some request has 4. `candidate_request`: never falls along the 2048 candidates of one req index; every request has 1 to 512 candidates, one exactly 512.
All inputs are finite; a program needn't handle non-finite values.
Results may differ from the reference program's by a relative error of at most 0.0056.
Values may be sent and summed in bfloat16 or wider, within the bound.
A program may use at most 128 MiB of HBM per device.

```python
import math
import jax
import jax.numpy as jnp
import numpy as np
from jax import lax

D = 1024
HEADS = 8
HD = 128
BLOCK = 128
MAXB = 4
CAP = 1
USERS_DEV = 8
CAND_DEV = 2048
REQ_DEV = 8
REQ_SHARDS = 8
REQUESTS = 64
USERS = 64
CANDS = 16384
TOKC = 512
TOTB = 24
MOSTC = 512
QW = 4096
KVW = 2048
HW = 1024


def with_ends(entries, stream_key, smallest, top_value):
    extent = entries.shape
    spot = [jax.random.randint(jax.random.fold_in(stream_key, axis), (), 0, extent[axis]) for axis in range(len(extent))]
    entries = entries.at[tuple(spot)].set(smallest)
    longest = extent.index(max(extent))
    spot[longest] = (spot[longest] + 1) % extent[longest]
    return entries.at[tuple(spot)].set(top_value)


def shard_levels(key, shape, pieces, low, high):
    def one(dim, blocks):
        steps = jax.random.uniform(jax.random.fold_in(jax.random.fold_in(key, 6), dim), (blocks,), jnp.float32, low / len(pieces), high / len(pieces))
        return jnp.repeat(jnp.exp(steps), shape[dim] // blocks).reshape((-1,) + (1,) * (len(shape) - dim - 1))

    gain = one(*pieces[0])
    for cut in pieces[1:]:
        gain = gain * one(*cut)
    return gain


def length_profile(count, total, reach, slope):
    weights = [(1 << 20) // math.isqrt(rank ** slope) + 1 for rank in range(2, count + 1)]
    spare, holding = total - reach - (count - 1), [1] * (count - 1)
    while spare > 0:
        movable = [i for i in range(count - 1) if holding[i] < reach]
        mass, budget = sum([weights[i] for i in movable]), spare
        for i in movable:
            addition = min(reach - holding[i], max(1, budget * weights[i] // mass), spare)
            holding[i] = holding[i] + addition
            spare = spare - addition
    return np.array([reach] + holding)


def ragged_sizes(key, amount, total, reach, slope):
    if amount == 2:
        one = jax.random.randint(key, (), max(1, total - reach), min(reach, total - 1) + 1)
        return jnp.stack([one, total - one])
    sizes = jnp.asarray(length_profile(amount, total, reach, slope), jnp.int32)
    couples = (amount - 1) // 2
    source_of, taker = sizes[1:1 + 2 * couples:2], sizes[2:2 + 2 * couples:2]
    margin = jnp.minimum(source_of - 1, reach - taker)
    shifted = jax.random.randint(jax.random.fold_in(key, 1), (couples,), 0, 1 << 20) % (margin + 1)
    sizes = sizes.at[1:1 + 2 * couples:2].set(source_of - shifted).at[2:2 + 2 * couples:2].set(taker + shifted)
    return sizes[jax.random.permutation(jax.random.fold_in(key, 2), amount)]


def assign_block(rng, own, number, rows, number_of, top, reach, lean):
    sequence = jax.random.permutation(rng, number_of)
    crowded, ordinary = load_shares(number_of, rows * top, reach, lean, True), load_shares(number_of, rows * top, reach, lean, False)
    places = jnp.arange(number_of)

    def named(tallies, rotation):
        used = int((tallies > 0).sum())
        fixed = max(1, used // 4)
        shifted = fixed + (places - fixed + rotation * (used - fixed)) % max(1, number_of - fixed)
        return jnp.zeros((number_of,), jnp.int32).at[sequence[jnp.where(places < fixed, places, shifted)]].set(jnp.asarray(tallies, jnp.int32))

    tallies = jnp.where(number % 4 == 0, named(crowded, number // 4), named(ordinary, number - number // 4 - 1))
    mixed = jax.random.permutation(jax.random.fold_in(own, 3), number_of)
    giver, sink = mixed[0:number_of // 2 * 2:2], mixed[1:number_of // 2 * 2:2]
    margin = jnp.minimum(tallies[giver] - 1, reach - tallies[sink]) // 2
    margin = jnp.where((giver == sequence[0]) | (sink == sequence[0]) | (tallies[sink] == 0), 0, jnp.maximum(margin, 0))
    shifted = jax.random.randint(jax.random.fold_in(own, 4), (number_of // 2,), 0, 1 << 20) % (margin + 1)
    tallies = tallies.at[giver].add(-shifted).at[sink].add(shifted)
    items = jnp.searchsorted(jnp.cumsum(tallies), jnp.arange(rows * top), side="right").astype(jnp.int32)
    table = items.reshape(top, rows).T
    table = table[jax.random.permutation(jax.random.fold_in(own, 1), rows)]
    rotation = jax.random.randint(jax.random.fold_in(own, 2), (rows, 1), 0, top)
    return jnp.take_along_axis(table, (jnp.arange(top)[None, :] + rotation) % top, axis=1)


def load_shares(number_of, total, reach, slope, full):
    portions = [(1 << 20) // math.isqrt(grade ** slope) + 1 for grade in range(1, number_of + 1)]
    largest = reach if full else min(reach, max(-(-total // number_of), total * portions[0] // sum(portions)))
    least = 1 if total - largest >= number_of - 1 else 0
    holding, surplus = [largest] + [least] * (number_of - 1), total - largest - least * (number_of - 1)
    while surplus > 0:
        free = [i for i in range(1, number_of) if holding[i] < largest] or [i for i in range(1, number_of) if holding[i] < reach]
        mass, left = sum([portions[i] for i in free]), surplus
        for i in free:
            extra = min(reach - holding[i], max(1, left * portions[i] // mass), surplus)
            holding[i] = holding[i] + extra
            surplus = surplus - extra
    return np.array(holding)


def centred(stream_key, dims, scale, reach, split=(), dtype=jnp.bfloat16):
    result = jax.random.normal(stream_key, dims, jnp.float32) * scale
    if len(split) > 0:
        result = shard_levels(stream_key, dims, split, -0.22, 0.18) * result
    return jnp.clip(result, min=-reach, max=reach).astype(dtype)


def setup_inputs(seed: int = 0, part: int = 0) -> dict:
    keys = jax.random.split(jax.random.key(seed), 9)
    own_keys = jax.random.split(jax.random.fold_in(keys[8], part), 9)
    candidates = centred(own_keys[0], (CANDS, D), 1.0, 6.0, ((0, 8),))
    candidate_request = jax.vmap(lambda own: jnp.searchsorted(jnp.cumsum(ragged_sizes(own, REQ_DEV, CAND_DEV, MOSTC, 1)), jnp.arange(CAND_DEV), side="right"))(jax.random.split(own_keys[1], REQ_SHARDS)).reshape((REQ_SHARDS, CAND_DEV)).astype(jnp.int32)
    request_owner_keys = jax.random.split(jax.random.fold_in(own_keys[2], 1), REQUESTS // REQ_DEV)
    request_owner_turns = jax.random.permutation(jax.random.fold_in(own_keys[2], 3), REQUESTS // REQ_DEV)
    request_owner = jax.vmap(lambda own, number: assign_block(jax.random.fold_in(own_keys[2], 2), own, number, REQ_DEV, REQ_SHARDS, 1, CAP, 0))(request_owner_keys, request_owner_turns).reshape((REQUESTS, 1))
    request_user = with_ends(jax.random.randint(own_keys[3], (REQUESTS,), 0, USERS_DEV), jax.random.fold_in(own_keys[3], 1), 0, USERS_DEV - 1).astype(jnp.int32)
    request_blocks = jax.vmap(lambda own: ragged_sizes(own, REQ_DEV, TOTB, MAXB, 2))(jax.random.split(own_keys[4], REQ_SHARDS)).reshape((REQ_SHARDS, REQ_DEV)).astype(jnp.int32)
    kv_cache = centred(own_keys[5], (USERS, TOKC, KVW), 1.0, 6.0, ((0, 8), (2, 2)))
    w_in = centred(keys[6], (D, QW), D ** -0.5, 0.1875, ((1, 2),))
    w_out = centred(keys[7], (HW, D), HW ** -0.5, 0.1875, ((0, 2),))
    return {"candidates": candidates, "candidate_request": candidate_request, "request_owner": request_owner, "request_user": request_user, "request_blocks": request_blocks, "kv_cache": kv_cache, "w_in": w_in, "w_out": w_out}


EPSILON = 1e-05

def normalize(values):
    center = values - lax.optimization_barrier(jnp.mean(values, axis=-1, keepdims=True))
    spread = lax.optimization_barrier(jnp.mean(center * center, axis=-1, keepdims=True))
    return center * lax.rsqrt(spread + EPSILON)

def reference(candidates, candidate_request, request_owner, request_user, request_blocks, kv_cache, w_in, w_out):
    normed = normalize(candidates.astype(jnp.float32)).astype(jnp.bfloat16)
    projected = jax.nn.silu(jnp.dot(normed, w_in, preferred_element_type=jnp.float32)).astype(jnp.bfloat16)
    projected = projected.reshape(REQ_SHARDS, CAND_DEV, HEADS, 4, HD)
    owner_rows = request_owner[:, 0].reshape(REQ_SHARDS, REQ_DEV)
    user_rows = request_user.reshape(REQ_SHARDS, REQ_DEV)
    scale = 1.0 / math.sqrt(HD)
    token_pos = jnp.arange(TOKC).astype(jnp.int32)

    def one_shard(items):
        proj, segment, owners, local_users, lengths = items
        gates = proj[:, :, 0].astype(jnp.float32)
        values_own = proj[:, :, 1].astype(jnp.float32)
        queries = proj[:, :, 2].astype(jnp.float32)
        keys_own = proj[:, :, 3].astype(jnp.float32)
        self_score = lax.optimization_barrier(jnp.sum(queries * keys_own, axis=-1)) * scale
        attended = jax.nn.silu(self_score)[..., None] * values_own

        def add_request(request, total):
            request = jnp.asarray(request).astype(jnp.int32)
            start = jnp.sum((segment < request).astype(jnp.int32))
            start = jnp.clip(start, 0, CAND_DEV - MOSTC).astype(jnp.int32)
            rows_q = lax.dynamic_slice_in_dim(queries, start, MOSTC, 0)
            rows_seg = lax.dynamic_slice_in_dim(segment, start, MOSTC, 0)
            global_user = (owners[request] * USERS_DEV + local_users[request]).astype(jnp.int32)
            cached = lax.dynamic_index_in_dim(kv_cache, global_user, 0, keepdims=False)
            cached = cached.reshape(TOKC, HEADS, 2, HD).astype(jnp.float32)
            live = token_pos < lengths[request] * BLOCK
            scores = jnp.einsum('whd,thd->hwt', rows_q, cached[:, :, 0]) * scale
            weights = jnp.where(live[None, None, :], jax.nn.silu(scores), 0.0).astype(jnp.bfloat16)
            weights = lax.optimization_barrier(weights).astype(jnp.float32)
            mixed = jnp.einsum('hwt,thd->whd', weights, cached[:, :, 1])
            mixed = jnp.where((rows_seg == request)[:, None, None], mixed, 0.0)
            current = lax.dynamic_slice_in_dim(total, start, MOSTC, 0)
            return lax.dynamic_update_slice_in_dim(total, current + mixed, start, 0)
        attended = lax.fori_loop(0, REQ_DEV, add_request, attended)
        gated = (normalize(attended) * gates).astype(jnp.bfloat16)
        return gated.reshape(CAND_DEV, HW)
    gated = lax.map(one_shard, (projected, candidate_request, owner_rows, user_rows, request_blocks))
    output = jnp.dot(gated.reshape(CANDS, HW), w_out, preferred_element_type=jnp.float32)
    return (output + candidates.astype(jnp.float32)).astype(jnp.bfloat16)
```

```python
import math

import jax
import jax.numpy as jnp
from jax import lax
from jax.experimental import pallas as pl
from jax.experimental.pallas import tpu as pltpu
from jax.sharding import PartitionSpec as P

HD = 128
BLOCK = 128
MOSTC = 512
EPSILON = 1e-05
VMEM_LIMIT = 60000 * 1024


def silu_half(y):
    return y + y * jnp.tanh(y)


def normalize(values):
    center = values - jnp.mean(values, axis=-1, keepdims=True)
    spread = jnp.mean(center * center, axis=-1, keepdims=True)
    return center * lax.rsqrt(spread + EPSILON)


def project_kernel(cand_ref, w_ref, q_ref, g_ref, self_ref):
    heads = q_ref.shape[1] // HD
    scale = 1.0 / math.sqrt(HD)
    normed = normalize(cand_ref[...].astype(jnp.float32)).astype(jnp.bfloat16)
    for h in range(heads):
        part = jnp.dot(
            normed, w_ref[:, h * 4 * HD : (h + 1) * 4 * HD], preferred_element_type=jnp.float32
        )
        part = silu_half(0.5 * part).astype(jnp.bfloat16)
        columns = slice(h * HD, (h + 1) * HD)
        query = part[:, 2 * HD : 3 * HD]
        g_ref[:, columns] = part[:, :HD]
        q_ref[:, columns] = query
        score = jnp.sum(
            query.astype(jnp.float32) * part[:, 3 * HD :].astype(jnp.float32), axis=-1, keepdims=True
        )
        weight = silu_half(score * (0.5 * scale))
        self_ref[:, columns] = weight * part[:, HD : 2 * HD].astype(jnp.float32)


def project(candidates, w_in):
    rows, width = candidates.shape
    columns = w_in.shape[1] // 4
    tile = min(256, rows)
    return pl.pallas_call(
        project_kernel,
        grid=(rows // tile,),
        in_specs=[
            pl.BlockSpec((tile, width), lambda i: (i, 0)),
            pl.BlockSpec(w_in.shape, lambda i: (0, 0), pipeline_mode=pl.Buffered(1)),
        ],
        out_specs=[pl.BlockSpec((tile, columns), lambda i: (i, 0))] * 3,
        out_shape=[
            jax.ShapeDtypeStruct((rows, columns), jnp.bfloat16),
            jax.ShapeDtypeStruct((rows, columns), jnp.bfloat16),
            jax.ShapeDtypeStruct((rows, columns), jnp.float32),
        ],
        cost_estimate=pl.CostEstimate(
            flops=2 * rows * width * 4 * columns,
            bytes_accessed=2 * (rows * width + width * 4 * columns + 4 * rows * columns),
            transcendentals=rows * 4 * columns,
        ),
        compiler_params=pltpu.CompilerParams(vmem_limit_bytes=VMEM_LIMIT),
        name="project",
    )(candidates, w_in)


def attend_kernel(tile, info, q_ref, g_ref, self_ref, kv_ref, w_ref, own_ref, *rest):
    peer_refs, gated = rest[:-1], rest[-1]
    window, width = q_ref.shape
    heads = width // HD
    tokens = kv_ref.shape[1]
    columns = own_ref.shape[1]
    scale = 1.0 / math.sqrt(HD)
    live = lax.broadcasted_iota(jnp.int32, (1, tokens), 1) < info[3]
    for t in range(window // tile):
        rows = slice(t * tile, (t + 1) * tile)
        for h in range(heads):
            cols = slice(h * HD, (h + 1) * HD)
            keys = kv_ref[0, :, 2 * h * HD : (2 * h + 1) * HD]
            values = kv_ref[0, :, (2 * h + 1) * HD : (2 * h + 2) * HD]
            scores = lax.dot_general(
                q_ref[rows, cols], keys, (((1,), (1,)), ((), ())), preferred_element_type=jnp.float32
            )
            weights = silu_half(scores * (0.5 * scale))
            weights = jnp.where(live, weights, 0.0).astype(jnp.bfloat16)
            mixed = jnp.dot(weights, values, preferred_element_type=jnp.float32)
            normed = normalize(self_ref[rows, cols] + mixed)
            gated[rows, cols] = (normed * g_ref[rows, cols].astype(jnp.float32)).astype(jnp.bfloat16)
        partial = jnp.dot(gated[rows, :], w_ref[...], preferred_element_type=jnp.float32)
        own_ref[rows, :] = partial[:, :columns]
        for k, peer_ref in enumerate(peer_refs, 1):
            peer_ref[rows, :] = partial[:, k * columns : (k + 1) * columns].astype(jnp.bfloat16)


def attend(info, queries, gates, selfs, cached, w_turned, window, ways):
    width = queries.shape[1]
    columns = w_turned.shape[1] // ways
    tokens, kvw = cached.shape[1:]
    tile = window // 3 if window % 48 == 0 else window
    rows = lambda i, info: (pl.multiple_of(info[0], 16), 0)
    view = pl.BlockSpec((pl.Element(window), pl.Element(width)), rows)
    whole = pl.BlockSpec((window, columns), lambda i, info: (0, 0))
    return pl.pallas_call(
        lambda *refs: attend_kernel(tile, *refs),
        grid_spec=pltpu.PrefetchScalarGridSpec(
            num_scalar_prefetch=1,
            grid=(1,),
            in_specs=[
                view,
                view,
                view,
                pl.BlockSpec((1, tokens, kvw), lambda i, info: (0, 0, 0)),
                pl.BlockSpec(w_turned.shape, lambda i, info: (0, 0)),
            ],
            out_specs=[whole] * ways,
            scratch_shapes=[pltpu.VMEM((window, width), jnp.bfloat16)],
        ),
        out_shape=[jax.ShapeDtypeStruct((window, columns), jnp.float32)]
        + [jax.ShapeDtypeStruct((window, columns), jnp.bfloat16)] * (ways - 1),
        cost_estimate=pl.CostEstimate(
            flops=4 * window * tokens * width + 2 * window * width * ways * columns,
            bytes_accessed=8 * window * width + 2 * tokens * kvw + 6 * window * ways * columns,
            transcendentals=window * tokens * width // HD,
        ),
        compiler_params=pltpu.CompilerParams(vmem_limit_bytes=VMEM_LIMIT),
        name="attend",
    )(info, queries, gates, selfs, cached, w_turned)


def finish_kernel(info, total_ref, own_ref, *rest):
    peer_refs, out_ref = rest[:-1], rest[-1]
    window = own_ref.shape[0]
    position = info[0] + lax.broadcasted_iota(jnp.int32, (window, 1), 0)
    mine = jnp.logical_and(position >= info[1], position < info[2])
    before = total_ref[...].astype(jnp.float32)
    total = own_ref[...]
    for peer_ref in peer_refs:
        total = total + peer_ref[...].astype(jnp.float32)
    out_ref[...] = jnp.where(mine, total + before, before).astype(out_ref.dtype)


def finish(info, total, own, peers):
    window, columns = own.shape
    rows = lambda i, info: (pl.multiple_of(info[0], 16), 0)
    view = pl.BlockSpec((pl.Element(window), pl.Element(columns)), rows)
    whole = pl.BlockSpec((window, columns), lambda i, info: (0, 0))
    return pl.pallas_call(
        finish_kernel,
        grid_spec=pltpu.PrefetchScalarGridSpec(
            num_scalar_prefetch=1,
            grid=(1,),
            in_specs=[view] + [whole] * (1 + len(peers)),
            out_specs=view,
        ),
        out_shape=jax.ShapeDtypeStruct(total.shape, total.dtype),
        input_output_aliases={1: 0},
        cost_estimate=pl.CostEstimate(
            flops=3 * window * columns, bytes_accessed=10 * window * columns, transcendentals=0
        ),
        compiler_params=pltpu.CompilerParams(vmem_limit_bytes=VMEM_LIMIT),
        name="finish",
    )(info, total, own, *peers)


def exchange_order(count):
    return sorted(range(count), key=lambda m: (-(m.bit_length()), m))


def per_device(
    candidates,
    candidate_request,
    request_owner,
    request_user,
    request_blocks,
    kv_cache,
    w_in,
    w_out,
):
    rows, width = candidates.shape
    count = lax.axis_size("req")
    ways = lax.axis_size("head")
    myself = lax.axis_index("req")
    side = lax.axis_index("head")
    columns = width // ways
    window = min(MOSTC + 16, rows)
    owners = request_owner[:, 0]
    everyone = jnp.arange(count, dtype=jnp.int32)
    names = (owners[None, :] == everyone[:, None]).astype(jnp.int32)
    wanted = jnp.sum(names * request_user[None, :], axis=1)
    asked = lax.all_gather(wanted, "req", axis=0, tiled=False)[:, myself]

    segment = candidate_request[0]
    served = jnp.sum(names * jnp.arange(owners.shape[0], dtype=jnp.int32)[None, :], axis=1)
    starts = jnp.sum((segment[None, :] < served[:, None]).astype(jnp.int32), axis=1)
    ends = jnp.sum((segment[None, :] <= served[:, None]).astype(jnp.int32), axis=1)
    exists = jnp.sum(names, axis=1) > 0
    ends = jnp.where(exists, ends, starts)
    live = jnp.sum(names * request_blocks[0][None, :], axis=1) * BLOCK
    firsts = jnp.minimum(starts // 16 * 16, rows - window)
    infos = jnp.stack([firsts, starts, ends, live], axis=1)

    order = exchange_order(count)
    arrived = {}
    for m in order:
        partner = jnp.bitwise_xor(myself, m)
        picked = lax.dynamic_slice_in_dim(kv_cache, asked[partner], 1, 0)
        if m:
            picked = lax.ppermute(picked, "req", [(i, i ^ m) for i in range(count)])
        arrived[m] = picked

    queries, gates, selfs = project(candidates, w_in)
    turned = jnp.concatenate(
        [
            lax.dynamic_slice_in_dim(w_out, ((side + k) % ways) * columns, columns, 1)
            for k in range(ways)
        ],
        axis=1,
    )
    ranked = lax.dynamic_slice_in_dim(candidates, side * columns, columns, 1)
    sequence = [0] + [m for m in reversed(order) if m == 1] + [m for m in order if m > 1]
    previous = None
    parts = []
    for m in sequence:
        info = infos[jnp.bitwise_xor(myself, m)]
        if previous is not None:
            info, previous = lax.optimization_barrier((info, previous))
        own, *peers = attend(info, queries, gates, selfs, arrived[m], turned, window, ways)
        previous = own
        landed = [
            lax.ppermute(peer, "head", [(i, (i + k) % ways) for i in range(ways)])
            for k, peer in enumerate(peers, 1)
        ]
        parts.append((info, own, landed))
    for info, own, landed in parts:
        ranked = finish(info, ranked, own, landed)
    return ranked


def solution(mesh):
    placed = (
        P(("groups", "req", "rep"), None),
        P(("groups", "req"), "rep"),
        P(("groups", "req"), None),
        P(("groups", "req")),
        P(("groups", "req"), None),
        P(("groups", "req"), None, "head"),
        P(None, "head"),
        P("head", None),
    )
    return jax.shard_map(
        per_device,
        mesh=mesh,
        in_specs=placed,
        out_specs=P(("groups", "req", "rep"), "head"),
        check_vma=False,
    )
```

```python
import math

import jax
import jax.numpy as jnp
from jax import lax
from jax.experimental import pallas as pl
from jax.experimental.pallas import tpu as pltpu
from jax.sharding import PartitionSpec as P

HD = 128
BLOCK = 128
MOSTC = 512
EPSILON = 1e-05
VMEM_LIMIT = 58 * 1024 * 1024


def silu_half(y):
    return y + y * jnp.tanh(y)


def normalize(values):
    center = values - jnp.mean(values, axis=-1, keepdims=True)
    spread = jnp.mean(center * center, axis=-1, keepdims=True)
    return center * lax.rsqrt(spread + EPSILON)


def project_kernel(cand_ref, w_ref, q_ref, g_ref, self_ref):
    heads = q_ref.shape[1] // HD
    scale = 1.0 / math.sqrt(HD)
    normed = normalize(cand_ref[...].astype(jnp.float32)).astype(jnp.bfloat16)
    for h in range(heads):
        part = jnp.dot(
            normed, w_ref[:, h * 4 * HD : (h + 1) * 4 * HD], preferred_element_type=jnp.float32
        )
        part = silu_half(0.5 * part).astype(jnp.bfloat16)
        columns = slice(h * HD, (h + 1) * HD)
        query = part[:, 2 * HD : 3 * HD]
        g_ref[:, columns] = part[:, :HD]
        q_ref[:, columns] = query
        score = jnp.sum(
            query.astype(jnp.float32) * part[:, 3 * HD :].astype(jnp.float32), axis=-1, keepdims=True
        )
        weight = silu_half(score * (0.5 * scale))
        self_ref[:, columns] = weight * part[:, HD : 2 * HD].astype(jnp.float32)


def project(candidates, w_in):
    rows, width = candidates.shape
    columns = w_in.shape[1] // 4
    tile = min(256, rows)
    return pl.pallas_call(
        project_kernel,
        grid=(rows // tile,),
        in_specs=[
            pl.BlockSpec((tile, width), lambda i: (i, 0)),
            pl.BlockSpec(w_in.shape, lambda i: (0, 0), pipeline_mode=pl.Buffered(1)),
        ],
        out_specs=[pl.BlockSpec((tile, columns), lambda i: (i, 0))] * 3,
        out_shape=[
            jax.ShapeDtypeStruct((rows, columns), jnp.bfloat16),
            jax.ShapeDtypeStruct((rows, columns), jnp.bfloat16),
            jax.ShapeDtypeStruct((rows, columns), jnp.float32),
        ],
        cost_estimate=pl.CostEstimate(
            flops=2 * rows * width * 4 * columns,
            bytes_accessed=2 * (rows * width + width * 4 * columns + 4 * rows * columns),
            transcendentals=rows * 4 * columns,
        ),
        compiler_params=pltpu.CompilerParams(vmem_limit_bytes=VMEM_LIMIT),
        name="project",
    )(candidates, w_in)


def attend_kernel(tile, m, place, infos, q_ref, g_ref, self_ref, kv_ref, w_ref, own_ref, *rest):
    peer_refs, gated = rest[:-1], rest[-1]
    window, width = q_ref.shape
    heads = width // HD
    tokens = kv_ref.shape[1]
    columns = own_ref.shape[1]
    scale = 1.0 / math.sqrt(HD)
    who = jnp.bitwise_xor(place[0], m)
    first, start, end = infos[0, who], infos[1, who], infos[2, who]
    live = lax.broadcasted_iota(jnp.int32, (1, tokens), 1) < infos[3, who]

    def one_tile(t):
        rows = slice(t * tile, (t + 1) * tile)
        for h in range(heads):
            cols = slice(h * HD, (h + 1) * HD)
            keys = kv_ref[0, :, 2 * h * HD : (2 * h + 1) * HD]
            values = kv_ref[0, :, (2 * h + 1) * HD : (2 * h + 2) * HD]
            scores = lax.dot_general(
                q_ref[rows, cols], keys, (((1,), (1,)), ((), ())), preferred_element_type=jnp.float32
            )
            weights = silu_half(scores * (0.5 * scale))
            weights = jnp.where(live, weights, 0.0).astype(jnp.bfloat16)
            mixed = jnp.dot(weights, values, preferred_element_type=jnp.float32)
            normed = normalize(self_ref[rows, cols] + mixed)
            gated[rows, cols] = (normed * g_ref[rows, cols].astype(jnp.float32)).astype(jnp.bfloat16)
        partial = jnp.dot(gated[rows, :], w_ref[...], preferred_element_type=jnp.float32)
        own_ref[rows, :] = partial[:, :columns]
        for k, peer_ref in enumerate(peer_refs, 1):
            peer_ref[rows, :] = partial[:, k * columns : (k + 1) * columns].astype(jnp.bfloat16)

    for t in range(window // tile):
        low = first + t * tile
        pl.when(jnp.logical_and(low < end, low + tile > start))(lambda t=t: one_tile(t))


def attend(place, infos, m, queries, gates, selfs, cached, w_turned, window, ways):
    width = queries.shape[1]
    columns = w_turned.shape[1] // ways
    tokens, kvw = cached.shape[1:]
    tile = window // 3 if window % 48 == 0 else window
    rows = lambda i, place, infos: (
        pl.multiple_of(infos[0, jnp.bitwise_xor(place[0], m)], 16),
        0,
    )
    view = pl.BlockSpec((pl.Element(window), pl.Element(width)), rows)
    whole = pl.BlockSpec((window, columns), lambda i, place, infos: (0, 0))
    return pl.pallas_call(
        lambda *refs: attend_kernel(tile, m, *refs),
        grid_spec=pltpu.PrefetchScalarGridSpec(
            num_scalar_prefetch=2,
            grid=(1,),
            in_specs=[
                view,
                view,
                view,
                pl.BlockSpec((1, tokens, kvw), lambda i, place, infos: (0, 0, 0)),
                pl.BlockSpec(w_turned.shape, lambda i, place, infos: (0, 0)),
            ],
            out_specs=[whole] * ways,
            scratch_shapes=[pltpu.VMEM((window, width), jnp.bfloat16)],
        ),
        out_shape=[jax.ShapeDtypeStruct((window, columns), jnp.float32)]
        + [jax.ShapeDtypeStruct((window, columns), jnp.bfloat16)] * (ways - 1),
        cost_estimate=pl.CostEstimate(
            flops=4 * window * tokens * width + 2 * window * width * ways * columns,
            bytes_accessed=8 * window * width + 2 * tokens * kvw + 6 * window * ways * columns,
            transcendentals=window * tokens * width // HD,
        ),
        compiler_params=pltpu.CompilerParams(vmem_limit_bytes=VMEM_LIMIT),
        name="attend",
    )(place, infos, queries, gates, selfs, cached, w_turned)


def finish_kernel(m, ways, place, infos, total_ref, own_ref, *rest):
    peer_refs, out_ref = rest[: ways - 1], rest[-1]
    who = jnp.bitwise_xor(place[0], m)
    window = own_ref.shape[0]
    position = infos[0, who] + lax.broadcasted_iota(jnp.int32, (window, 1), 0)
    mine = jnp.logical_and(position >= infos[1, who], position < infos[2, who])
    before = total_ref[...].astype(jnp.float32)
    total = own_ref[...]
    for peer_ref in peer_refs:
        total = total + peer_ref[...].astype(jnp.float32)
    out_ref[...] = jnp.where(mine, total + before, before).astype(out_ref.dtype)


def finish(place, infos, m, own, peers, total, after=None):
    window, columns = own.shape
    late = [] if after is None else [after]
    rows = lambda i, place, infos: (
        pl.multiple_of(infos[0, jnp.bitwise_xor(place[0], m)], 16),
        0,
    )
    view = pl.BlockSpec((pl.Element(window), pl.Element(columns)), rows)
    whole = pl.BlockSpec((window, columns), lambda i, place, infos: (0, 0))
    return pl.pallas_call(
        lambda *refs: finish_kernel(m, 1 + len(peers), *refs),
        grid_spec=pltpu.PrefetchScalarGridSpec(
            num_scalar_prefetch=2,
            grid=(1,),
            in_specs=[view]
            + [whole] * (1 + len(peers))
            + [pl.BlockSpec(memory_space=pl.ANY)] * len(late),
            out_specs=view,
        ),
        out_shape=jax.ShapeDtypeStruct(total.shape, total.dtype),
        input_output_aliases={2: 0},
        cost_estimate=pl.CostEstimate(
            flops=3 * window * columns, bytes_accessed=10 * window * columns, transcendentals=0
        ),
        compiler_params=pltpu.CompilerParams(vmem_limit_bytes=VMEM_LIMIT),
        name="finish",
    )(place, infos, total, own, *peers, *late)


def pick_kernel(place, table, kv_ref, *rest):
    rest[-1][...] = kv_ref[...]


def pick(place, table, kv_cache, m, after):
    user = lambda i, place, table: (table[jnp.bitwise_xor(place[0], m), place[0]], 0, 0)
    block = (1,) + kv_cache.shape[1:]
    return pl.pallas_call(
        pick_kernel,
        grid_spec=pltpu.PrefetchScalarGridSpec(
            num_scalar_prefetch=2,
            grid=(1,),
            in_specs=[pl.BlockSpec(block, user)] + [pl.BlockSpec(memory_space=pl.ANY)] * len(after),
            out_specs=pl.BlockSpec(block, lambda i, place, table: (0, 0, 0)),
        ),
        out_shape=jax.ShapeDtypeStruct(block, kv_cache.dtype),
        compiler_params=pltpu.CompilerParams(vmem_limit_bytes=VMEM_LIMIT),
        name="pick",
    )(place, table, kv_cache, *after)


def exchange_order(count):
    far = [m for m in range(count) if 2 * m >= count][::-1]
    near = [m for m in range(2, count) if 2 * m < count][::-1]
    order = []
    while far or near:
        order += far[:1] + (near[:1] if len(far) > 2 or not far else [])
        near = near[1:] if len(far) > 2 or not far else near
        far = far[1:]
    return order


def per_device(
    candidates,
    candidate_request,
    request_owner,
    request_user,
    request_blocks,
    kv_cache,
    w_in,
    w_out,
):
    rows, width = candidates.shape
    count = lax.axis_size("req")
    ways = lax.axis_size("head")
    myself = lax.axis_index("req")
    side = lax.axis_index("head")
    columns = width // ways
    window = min(MOSTC + 16, rows)
    owners = request_owner[:, 0]
    everyone = jnp.arange(count, dtype=jnp.int32)
    names = (owners[None, :] == everyone[:, None]).astype(jnp.int32)
    wanted = jnp.sum(names * request_user[None, :], axis=1)
    table = lax.all_gather(wanted, "req", axis=0, tiled=False)
    place = myself[None].astype(jnp.int32)

    order = exchange_order(count)
    arrived = {}
    after = []
    for m in order + [1, 0]:
        picked = pick(place, table, kv_cache, m, after)
        after = [picked]
        if m:
            picked = lax.ppermute(picked, "req", [(i, i ^ m) for i in range(count)])
        arrived[m] = picked

    segment = candidate_request[0]
    served = jnp.sum(names * jnp.arange(owners.shape[0], dtype=jnp.int32)[None, :], axis=1)
    starts = jnp.sum((segment[None, :] < served[:, None]).astype(jnp.int32), axis=1)
    ends = jnp.sum((segment[None, :] <= served[:, None]).astype(jnp.int32), axis=1)
    exists = jnp.sum(names, axis=1) > 0
    ends = jnp.where(exists, ends, starts)
    live = jnp.sum(names * request_blocks[0][None, :], axis=1) * BLOCK
    firsts = jnp.minimum(starts // 16 * 16, rows - window)
    infos = jnp.stack([firsts, starts, ends, live])

    queries, gates, selfs = project(candidates, w_in)
    turned = jnp.concatenate(
        [
            lax.dynamic_slice_in_dim(w_out, ((side + k) % ways) * columns, columns, 1)
            for k in range(ways)
        ],
        axis=1,
    )
    ranked = lax.dynamic_slice_in_dim(candidates, side * columns, columns, 1)
    sequence = [0, 1] + order
    pending = []
    ready = []
    for m in sequence:
        if ready:
            table_in, *ready = lax.optimization_barrier((infos, *ready))
        else:
            table_in = infos
        own, *peers = attend(
            place, table_in, m, queries, gates, selfs, arrived[m], turned, window, ways
        )
        landed = [
            lax.ppermute(peer, "head", [(i, (i + k) % ways) for i in range(ways)])
            for k, peer in enumerate(peers, 1)
        ]
        if pending:
            ranked = finish(place, infos, *pending.pop(), ranked, after=own)
        pending.append((m, own, landed))
        ready = [own, ranked]
    return finish(place, infos, *pending.pop(), ranked)


def solution(mesh):
    placed = (
        P(("groups", "req", "rep"), None),
        P(("groups", "req"), "rep"),
        P(("groups", "req"), None),
        P(("groups", "req")),
        P(("groups", "req"), None),
        P(("groups", "req"), None, "head"),
        P(None, "head"),
        P("head", None),
    )

    return jax.shard_map(
        per_device,
        mesh=mesh,
        in_specs=placed,
        out_specs=P(("groups", "req", "rep"), "head"),
        check_vma=False,
    )
```

```python
import math

import jax
import jax.numpy as jnp
from jax import lax
from jax.experimental import pallas as pl
from jax.experimental.pallas import tpu as pltpu
from jax.sharding import PartitionSpec as P

HD = 128
BLOCK = 128
MOSTC = 512
EPSILON = 1e-05
VMEM_LIMIT = 24000 * 1024


def silu_half(y):
    return y + y * jnp.tanh(y)


def normalize(values):
    center = values - jnp.mean(values, axis=-1, keepdims=True)
    spread = jnp.mean(center * center, axis=-1, keepdims=True)
    return center * lax.rsqrt(spread + EPSILON)


def project_kernel(cand_ref, w_ref, q_ref, g_ref, self_ref):
    heads = q_ref.shape[1] // HD
    scale = 1.0 / math.sqrt(HD)
    normed = normalize(cand_ref[...].astype(jnp.float32)).astype(jnp.bfloat16)
    for h in range(heads):
        part = jnp.dot(
            normed, w_ref[:, h * 4 * HD : (h + 1) * 4 * HD], preferred_element_type=jnp.float32
        )
        part = silu_half(0.5 * part).astype(jnp.bfloat16)
        columns = slice(h * HD, (h + 1) * HD)
        query = part[:, 2 * HD : 3 * HD]
        g_ref[:, columns] = part[:, :HD]
        q_ref[:, columns] = query
        score = jnp.sum(
            query.astype(jnp.float32) * part[:, 3 * HD :].astype(jnp.float32), axis=-1, keepdims=True
        )
        weight = silu_half(score * (0.5 * scale))
        self_ref[:, columns] = weight * part[:, HD : 2 * HD].astype(jnp.float32)


def project(candidates, w_in):
    rows, width = candidates.shape
    columns = w_in.shape[1] // 4
    tile = min(256, rows)
    return pl.pallas_call(
        project_kernel,
        grid=(rows // tile,),
        in_specs=[
            pl.BlockSpec((tile, width), lambda i: (i, 0)),
            pl.BlockSpec(w_in.shape, lambda i: (0, 0), pipeline_mode=pl.Buffered(1)),
        ],
        out_specs=[pl.BlockSpec((tile, columns), lambda i: (i, 0))] * 3,
        out_shape=[
            jax.ShapeDtypeStruct((rows, columns), jnp.bfloat16),
            jax.ShapeDtypeStruct((rows, columns), jnp.bfloat16),
            jax.ShapeDtypeStruct((rows, columns), jnp.float32),
        ],
        cost_estimate=pl.CostEstimate(
            flops=2 * rows * width * 4 * columns,
            bytes_accessed=2 * (rows * width + width * 4 * columns + 4 * rows * columns),
            transcendentals=rows * 4 * columns,
        ),
        compiler_params=pltpu.CompilerParams(vmem_limit_bytes=VMEM_LIMIT),
        name="project",
    )(candidates, w_in)


def window_rows(m, offset, tile):
    def index(i, place, infos):
        first = infos[0, jnp.bitwise_xor(place[0], m)]
        return pl.multiple_of(first + offset + i * tile, 16), 0

    return index


def attend_kernel(m, offset, place, infos, q_ref, g_ref, self_ref, kv_ref, w_ref, own_ref, *rest):
    peer_refs, gated = rest[:-1], rest[-1]
    tile, width = q_ref.shape
    heads = width // HD
    tokens = kv_ref.shape[1]
    columns = own_ref.shape[1]
    scale = 1.0 / math.sqrt(HD)
    who = jnp.bitwise_xor(place[0], m)
    low = infos[0, who] + offset + pl.program_id(0) * tile
    live = lax.broadcasted_iota(jnp.int32, (1, tokens), 1) < infos[3, who]

    @pl.when(jnp.logical_and(low < infos[2, who], low + tile > infos[1, who]))
    def _():
        for h in range(heads):
            cols = slice(h * HD, (h + 1) * HD)
            keys = kv_ref[0, :, 2 * h * HD : (2 * h + 1) * HD]
            values = kv_ref[0, :, (2 * h + 1) * HD : (2 * h + 2) * HD]
            scores = lax.dot_general(
                q_ref[:, cols], keys, (((1,), (1,)), ((), ())), preferred_element_type=jnp.float32
            )
            weights = silu_half(scores * (0.5 * scale))
            weights = jnp.where(live, weights, 0.0).astype(jnp.bfloat16)
            mixed = jnp.dot(weights, values, preferred_element_type=jnp.float32)
            normed = normalize(self_ref[:, cols] + mixed)
            gated[:, cols] = (normed * g_ref[:, cols].astype(jnp.float32)).astype(jnp.bfloat16)
        partial = jnp.dot(gated[...], w_ref[...], preferred_element_type=jnp.float32)
        own_ref[...] = partial[:, :columns]
        for k, peer_ref in enumerate(peer_refs, 1):
            peer_ref[...] = partial[:, k * columns : (k + 1) * columns].astype(jnp.bfloat16)


def attend(place, infos, m, offset, size, tile, queries, gates, selfs, cached, w_turned, ways):
    width = queries.shape[1]
    columns = w_turned.shape[1] // ways
    tokens, kvw = cached.shape[1:]
    view = pl.BlockSpec((pl.Element(tile), pl.Element(width)), window_rows(m, offset, tile))
    part = pl.BlockSpec((tile, columns), lambda i, place, infos: (i, 0))
    return pl.pallas_call(
        lambda *refs: attend_kernel(m, offset, *refs),
        grid_spec=pltpu.PrefetchScalarGridSpec(
            num_scalar_prefetch=2,
            grid=(size // tile,),
            in_specs=[
                view,
                view,
                view,
                pl.BlockSpec(
                    (1, tokens, kvw), lambda i, place, infos: (0, 0, 0), pipeline_mode=pl.Buffered(1)
                ),
                pl.BlockSpec(
                    w_turned.shape, lambda i, place, infos: (0, 0), pipeline_mode=pl.Buffered(1)
                ),
            ],
            out_specs=[part] * ways,
            scratch_shapes=[pltpu.VMEM((tile, width), jnp.bfloat16)],
        ),
        out_shape=[jax.ShapeDtypeStruct((size, columns), jnp.float32)]
        + [jax.ShapeDtypeStruct((size, columns), jnp.bfloat16)] * (ways - 1),
        cost_estimate=pl.CostEstimate(
            flops=4 * size * tokens * width + 2 * size * width * ways * columns,
            bytes_accessed=8 * size * width + 2 * tokens * kvw + 6 * size * ways * columns,
            transcendentals=size * tokens * width // HD,
        ),
        compiler_params=pltpu.CompilerParams(vmem_limit_bytes=VMEM_LIMIT),
        name="attend",
    )(place, infos, queries, gates, selfs, cached, w_turned)


def finish_kernel(m, offset, ways, place, infos, total_ref, own_ref, *rest):
    peer_refs, out_ref = rest[: ways - 1], rest[-1]
    who = jnp.bitwise_xor(place[0], m)
    tile = own_ref.shape[0]
    low = infos[0, who] + offset + pl.program_id(0) * tile
    position = low + lax.broadcasted_iota(jnp.int32, (tile, 1), 0)
    mine = jnp.logical_and(position >= infos[1, who], position < infos[2, who])
    before = total_ref[...].astype(jnp.float32)
    total = own_ref[...]
    for peer_ref in peer_refs:
        total = total + peer_ref[...].astype(jnp.float32)
    out_ref[...] = jnp.where(mine, total + before, before).astype(out_ref.dtype)


def finish(place, infos, m, offset, tile, own, peers, total, after=()):
    size, columns = own.shape
    view = pl.BlockSpec((pl.Element(tile), pl.Element(columns)), window_rows(m, offset, tile))
    part = pl.BlockSpec((tile, columns), lambda i, place, infos: (i, 0))
    return pl.pallas_call(
        lambda *refs: finish_kernel(m, offset, 1 + len(peers), *refs),
        grid_spec=pltpu.PrefetchScalarGridSpec(
            num_scalar_prefetch=2,
            grid=(size // tile,),
            in_specs=[view]
            + [part] * (1 + len(peers))
            + [pl.BlockSpec(memory_space=pl.ANY)] * len(after),
            out_specs=view,
        ),
        out_shape=jax.ShapeDtypeStruct(total.shape, total.dtype),
        input_output_aliases={2: 0},
        cost_estimate=pl.CostEstimate(
            flops=3 * size * columns, bytes_accessed=10 * size * columns, transcendentals=0
        ),
        compiler_params=pltpu.CompilerParams(vmem_limit_bytes=VMEM_LIMIT),
        name="finish",
    )(place, infos, total, own, *peers, *after)


def pick_kernel(place, table, kv_ref, *rest):
    rest[-1][...] = kv_ref[...]


def pick(place, table, kv_cache, m, after):
    user = lambda i, place, table: (table[jnp.bitwise_xor(place[0], m), place[0]], i, 0)
    tokens, kvw = kv_cache.shape[1:]
    block = (1, tokens // 4, kvw)
    return pl.pallas_call(
        pick_kernel,
        grid_spec=pltpu.PrefetchScalarGridSpec(
            num_scalar_prefetch=2,
            grid=(4,),
            in_specs=[pl.BlockSpec(block, user)] + [pl.BlockSpec(memory_space=pl.ANY)] * len(after),
            out_specs=pl.BlockSpec(block, lambda i, place, table: (0, i, 0)),
        ),
        out_shape=jax.ShapeDtypeStruct((1, tokens, kvw), kv_cache.dtype),
        compiler_params=pltpu.CompilerParams(vmem_limit_bytes=VMEM_LIMIT),
        name="pick",
    )(place, table, kv_cache, *after)


def exchange_order(count):
    far = [m for m in range(count) if 2 * m >= count][::-1]
    near = [m for m in range(2, count) if 2 * m < count][::-1]
    order = []
    while far or near:
        order += far[:1] + (near[:1] if len(far) > 2 or not far else [])
        near = near[1:] if len(far) > 2 or not far else near
        far = far[1:]
    return order


def per_device(
    candidates,
    candidate_request,
    request_owner,
    request_user,
    request_blocks,
    kv_cache,
    w_in,
    w_out,
):
    rows, width = candidates.shape
    count = lax.axis_size("req")
    ways = lax.axis_size("head")
    myself = lax.axis_index("req")
    side = lax.axis_index("head")
    columns = width // ways
    window = min(MOSTC + 16, rows)
    owners = request_owner[:, 0]
    everyone = jnp.arange(count, dtype=jnp.int32)
    names = (owners[None, :] == everyone[:, None]).astype(jnp.int32)
    wanted = jnp.sum(names * request_user[None, :], axis=1)
    table = lax.all_gather(wanted, "req", axis=0, tiled=False)
    place = myself[None].astype(jnp.int32)

    order = exchange_order(count)
    arrived = {}
    after = []
    for m in order + [1, 0]:
        picked = pick(place, table, kv_cache, m, after)
        after = [picked]
        if m:
            picked = lax.ppermute(picked, "req", [(i, i ^ m) for i in range(count)])
        arrived[m] = picked

    segment = candidate_request[0]
    served = jnp.sum(names * jnp.arange(owners.shape[0], dtype=jnp.int32)[None, :], axis=1)
    starts = jnp.sum((segment[None, :] < served[:, None]).astype(jnp.int32), axis=1)
    ends = jnp.sum((segment[None, :] <= served[:, None]).astype(jnp.int32), axis=1)
    exists = jnp.sum(names, axis=1) > 0
    ends = jnp.where(exists, ends, starts)
    live = jnp.sum(names * request_blocks[0][None, :], axis=1) * BLOCK
    firsts = jnp.minimum(starts // 16 * 16, rows - window)
    infos = jnp.stack([firsts, starts, ends, live])

    queries, gates, selfs = project(candidates, w_in)
    turned = jnp.concatenate(
        [
            lax.dynamic_slice_in_dim(w_out, ((side + k) % ways) * columns, columns, 1)
            for k in range(ways)
        ],
        axis=1,
    )
    ranked = lax.dynamic_slice_in_dim(candidates, side * columns, columns, 1)
    sequence = [0, 1] + order
    tile = window // 3 if window % 48 == 0 else window
    steps = [(m, 0, window) for m in sequence[:-1]]
    steps += [(sequence[-1], offset, tile) for offset in range(0, window, tile)]
    pending = []
    ready = []
    for m, offset, size in steps:
        current = infos
        if ready:
            current, *ready = lax.optimization_barrier((infos, *ready))
        own, *peers = attend(
            place, current, m, offset, size, tile, queries, gates, selfs, arrived[m], turned, ways
        )
        landed = [
            lax.ppermute(peer, "head", [(i, (i + k) % ways) for i in range(ways)])
            for k, peer in enumerate(peers, 1)
        ]
        ready = [own]
        if pending and m != sequence[-1]:
            ranked = finish(place, infos, *pending.pop(0), ranked, after=[own])
            ready = [own, ranked]
        pending.append((m, offset, tile, own, landed))
    for one in pending:
        ranked = finish(place, infos, *one, ranked, after=ready[:1])
    return ranked


def solution(mesh):
    placed = (
        P(("groups", "req", "rep"), None),
        P(("groups", "req"), "rep"),
        P(("groups", "req"), None),
        P(("groups", "req")),
        P(("groups", "req"), None),
        P(("groups", "req"), None, "head"),
        P(None, "head"),
        P("head", None),
    )

    return jax.shard_map(
        per_device,
        mesh=mesh,
        in_specs=placed,
        out_specs=P(("groups", "req", "rep"), "head"),
        check_vma=False,
    )
```

```python
import math

import jax
import jax.numpy as jnp
from jax import lax
from jax.experimental import pallas as pl
from jax.experimental.pallas import tpu as pltpu
from jax.sharding import PartitionSpec as P

HD = 128
BLOCK = 128
MOSTC = 512
EPSILON = 1e-05
VMEM_LIMIT = 24000 * 1024
PICK_VMEM_LIMIT = 58 * 1024 * 1024


def silu_half(y):
    return y + y * jnp.tanh(y)


def normalize(values):
    center = values - jnp.mean(values, axis=-1, keepdims=True)
    spread = jnp.mean(center * center, axis=-1, keepdims=True)
    return center * lax.rsqrt(spread + EPSILON)


def project_kernel(cand_ref, w_ref, q_ref, g_ref, self_ref):
    heads = q_ref.shape[1] // HD
    scale = 1.0 / math.sqrt(HD)
    normed = normalize(cand_ref[...].astype(jnp.float32)).astype(jnp.bfloat16)
    for h in range(heads):
        part = jnp.dot(
            normed, w_ref[:, h * 4 * HD : (h + 1) * 4 * HD], preferred_element_type=jnp.float32
        )
        part = silu_half(0.5 * part).astype(jnp.bfloat16)
        columns = slice(h * HD, (h + 1) * HD)
        query = part[:, 2 * HD : 3 * HD]
        g_ref[:, columns] = part[:, :HD]
        q_ref[:, columns] = query
        score = jnp.sum(
            query.astype(jnp.float32) * part[:, 3 * HD :].astype(jnp.float32), axis=-1, keepdims=True
        )
        weight = silu_half(score * (0.5 * scale))
        self_ref[:, columns] = weight * part[:, HD : 2 * HD].astype(jnp.float32)


def project(candidates, w_in):
    rows, width = candidates.shape
    columns = w_in.shape[1] // 4
    tile = min(256, rows)
    return pl.pallas_call(
        project_kernel,
        grid=(rows // tile,),
        in_specs=[
            pl.BlockSpec((tile, width), lambda i: (i, 0)),
            pl.BlockSpec(w_in.shape, lambda i: (0, 0), pipeline_mode=pl.Buffered(1)),
        ],
        out_specs=[pl.BlockSpec((tile, columns), lambda i: (i, 0))] * 3,
        out_shape=[
            jax.ShapeDtypeStruct((rows, columns), jnp.bfloat16),
            jax.ShapeDtypeStruct((rows, columns), jnp.bfloat16),
            jax.ShapeDtypeStruct((rows, columns), jnp.float32),
        ],
        cost_estimate=pl.CostEstimate(
            flops=2 * rows * width * 4 * columns,
            bytes_accessed=2 * (rows * width + width * 4 * columns + 4 * rows * columns),
            transcendentals=rows * 4 * columns,
        ),
        compiler_params=pltpu.CompilerParams(vmem_limit_bytes=VMEM_LIMIT),
        name="project",
    )(candidates, w_in)


def window_rows(m, offset, tile):
    def index(i, place, infos):
        first = infos[0, jnp.bitwise_xor(place[0], m)]
        return pl.multiple_of(first + offset + i * tile, 16), 0

    return index


def attend_kernel(m, offset, place, infos, q_ref, g_ref, self_ref, kv_ref, gated_ref):
    tile, width = q_ref.shape
    tokens = kv_ref.shape[1]
    scale = 1.0 / math.sqrt(HD)
    who = jnp.bitwise_xor(place[0], m)
    low = infos[0, who] + offset + pl.program_id(0) * tile
    live = lax.broadcasted_iota(jnp.int32, (1, tokens), 1) < infos[3, who]

    @pl.when(jnp.logical_and(low < infos[2, who], low + tile > infos[1, who]))
    def _():
        for h in range(width // HD):
            cols = slice(h * HD, (h + 1) * HD)
            keys = kv_ref[0, :, 2 * h * HD : (2 * h + 1) * HD]
            values = kv_ref[0, :, (2 * h + 1) * HD : (2 * h + 2) * HD]
            scores = lax.dot_general(
                q_ref[:, cols], keys, (((1,), (1,)), ((), ())), preferred_element_type=jnp.float32
            )
            weights = silu_half(scores * (0.5 * scale))
            weights = jnp.where(live, weights, 0.0).astype(jnp.bfloat16)
            mixed = jnp.dot(weights, values, preferred_element_type=jnp.float32)
            normed = normalize(self_ref[:, cols] + mixed)
            gated_ref[:, cols] = (normed * g_ref[:, cols].astype(jnp.float32)).astype(jnp.bfloat16)


def attend(place, infos, m, offset, size, tile, side, sides, queries, gates, selfs, cached):
    width = queries.shape[1] // sides
    tokens, kvw = cached.shape[1:]
    rows = window_rows(m, offset, tile)
    view = pl.BlockSpec(
        (pl.Element(tile), pl.Element(width)),
        lambda i, place, infos: (rows(i, place, infos)[0], side * width),
    )
    return pl.pallas_call(
        lambda *refs: attend_kernel(m, offset, *refs),
        grid_spec=pltpu.PrefetchScalarGridSpec(
            num_scalar_prefetch=2,
            grid=(size // tile,),
            in_specs=[
                view,
                view,
                view,
                pl.BlockSpec(
                    (1, tokens, kvw), lambda i, place, infos: (0, 0, 0), pipeline_mode=pl.Buffered(1)
                ),
            ],
            out_specs=pl.BlockSpec((tile, width), lambda i, place, infos: (i, 0)),
        ),
        out_shape=jax.ShapeDtypeStruct((size, width), jnp.bfloat16),
        cost_estimate=pl.CostEstimate(
            flops=4 * size * tokens * width,
            bytes_accessed=10 * size * width + 2 * tokens * kvw,
            transcendentals=size * tokens * width // HD,
        ),
        compiler_params=pltpu.CompilerParams(vmem_limit_bytes=VMEM_LIMIT),
        name="attend",
    )(place, infos, queries, gates, selfs, cached)


def finish_kernel(m, offset, slots, place, infos, total_ref, w_ref, *rest):
    gated_refs, out_ref = rest[: len(slots)], rest[-1]
    who = jnp.bitwise_xor(place[0], m)
    tile = total_ref.shape[0]
    low = infos[0, who] + offset + pl.program_id(0) * tile
    position = low + lax.broadcasted_iota(jnp.int32, (tile, 1), 0)
    mine = jnp.logical_and(position >= infos[1, who], position < infos[2, who])
    before = total_ref[...].astype(jnp.float32)
    total = before
    for (k, row), ref in zip(slots, gated_refs):
        total = total + jnp.dot(
            ref[...], w_ref[k, row : row + ref.shape[1], :], preferred_element_type=jnp.float32
        )
    out_ref[...] = jnp.where(mine, total, before).astype(out_ref.dtype)


def finish(place, infos, m, offset, size, tile, slots, gated, total, turned, after=()):
    columns = total.shape[1]
    view = pl.BlockSpec((pl.Element(tile), pl.Element(columns)), window_rows(m, offset, tile))
    blocks = [
        pl.BlockSpec((tile, g.shape[1]), lambda i, place, infos, skip=skip: (i + skip, 0))
        for g, skip in gated
    ]
    arrays = [g for g, _ in gated]
    work = sum(g.shape[1] for g in arrays)
    return pl.pallas_call(
        lambda *refs: finish_kernel(m, offset, slots, *refs),
        grid_spec=pltpu.PrefetchScalarGridSpec(
            num_scalar_prefetch=2,
            grid=(size // tile,),
            in_specs=[
                view,
                pl.BlockSpec(
                    turned.shape, lambda i, place, infos: (0, 0, 0), pipeline_mode=pl.Buffered(1)
                ),
            ]
            + blocks
            + [pl.BlockSpec(memory_space=pl.ANY)] * len(after),
            out_specs=view,
        ),
        out_shape=jax.ShapeDtypeStruct(total.shape, total.dtype),
        input_output_aliases={2: 0},
        cost_estimate=pl.CostEstimate(
            flops=2 * size * columns * work,
            bytes_accessed=4 * size * columns + 2 * size * work + 2 * work * columns,
            transcendentals=0,
        ),
        compiler_params=pltpu.CompilerParams(vmem_limit_bytes=VMEM_LIMIT),
        name="finish",
    )(place, infos, total, turned, *arrays, *after)


def pick_kernel(place, table, kv_ref, *rest):
    rest[-1][...] = kv_ref[...]


def pick(place, table, count, kv_cache, m, side, sides, after):
    user = lambda i, place, table: (table[jnp.bitwise_xor(place[0], m) * count + place[0]], i, side)
    tokens, kvw = kv_cache.shape[1], kv_cache.shape[2] // sides
    block = (1, tokens // 4, kvw)
    return pl.pallas_call(
        pick_kernel,
        grid_spec=pltpu.PrefetchScalarGridSpec(
            num_scalar_prefetch=2,
            grid=(4,),
            in_specs=[pl.BlockSpec(block, user)] + [pl.BlockSpec(memory_space=pl.ANY)] * len(after),
            out_specs=pl.BlockSpec(block, lambda i, place, table: (0, i, 0)),
        ),
        out_shape=jax.ShapeDtypeStruct((1, tokens, kvw), kv_cache.dtype),
        compiler_params=pltpu.CompilerParams(vmem_limit_bytes=PICK_VMEM_LIMIT),
        name="pick",
    )(place, table, kv_cache, *after)


def exchange_order(count):
    far = [m for m in range(count) if 2 * m >= count][::-1]
    near = [m for m in range(2, count) if 2 * m < count][::-1]
    order = []
    while far or near:
        order += far[:1] + (near[:1] if len(far) > 2 or not far else [])
        near = near[1:] if len(far) > 2 or not far else near
        far = far[1:]
    return order


def per_device(
    candidates,
    candidate_request,
    request_owner,
    request_user,
    request_blocks,
    kv_cache,
    w_in,
    w_out,
):
    rows, width = candidates.shape
    count = lax.axis_size("req")
    ways = lax.axis_size("head")
    myself = lax.axis_index("req")
    side = lax.axis_index("head")
    columns = width // ways
    window = min(MOSTC + 16, rows)
    owners = request_owner[:, 0]
    everyone = jnp.arange(count, dtype=jnp.int32)
    names = (owners[None, :] == everyone[:, None]).astype(jnp.int32)
    wanted = jnp.sum(names * request_user[None, :], axis=1)
    spread = jnp.where(everyone[:, None] == myself, wanted[None, :], 0)
    table = lax.psum(spread.reshape(-1), "req")
    place = myself[None].astype(jnp.int32)

    order = exchange_order(count)
    arrived = {}
    after = []
    last = order[-1]
    for m in order + [1, 0]:
        sides = 2 if m == last else 1
        arrived[m] = []
        for part in range(sides):
            picked = pick(place, table, count, kv_cache, m, part, sides, after)
            after = [picked]
            if m:
                picked = lax.ppermute(picked, "req", [(i, i ^ m) for i in range(count)])
            arrived[m].append(picked)

    segment = candidate_request[0]
    served = jnp.sum(names * jnp.arange(owners.shape[0], dtype=jnp.int32)[None, :], axis=1)
    starts = jnp.sum((segment[None, :] < served[:, None]).astype(jnp.int32), axis=1)
    ends = jnp.sum((segment[None, :] <= served[:, None]).astype(jnp.int32), axis=1)
    exists = jnp.sum(names, axis=1) > 0
    ends = jnp.where(exists, ends, starts)
    live = jnp.sum(names * request_blocks[0][None, :], axis=1) * BLOCK
    firsts = jnp.minimum(starts // 16 * 16, rows - window)
    infos = jnp.stack([firsts, starts, ends, live])

    queries, gates, selfs = project(candidates, w_in)

    def to_peer(value, k):
        return lax.ppermute(value, "head", [(i, (i + k) % ways) for i in range(ways)])

    turned = []
    for k in range(ways):
        piece = lax.dynamic_slice_in_dim(w_out, ((side + k) % ways) * columns, columns, 1)
        turned.append(to_peer(piece, k) if k else piece)
    turned = jnp.stack(turned)
    ranked = lax.dynamic_slice_in_dim(candidates, side * columns, columns, 1)
    sequence = [0, 1] + order
    tile = window // 3 if window % 48 == 0 else window
    half = w_out.shape[0] // 2

    def run(m, offset, size, part, sides, ready):
        current = infos
        if ready:
            current, *ready = lax.optimization_barrier((infos, *ready))
        gated = attend(
            place, current, m, offset, size, tile, part, sides, queries, gates, selfs, arrived[m][part]
        )
        return [gated] + [to_peer(gated, k) for k in range(1, ways)]

    def add(m, offset, size, slots, gated, ranked, after):
        return finish(place, infos, m, offset, size, tile, slots, gated, ranked, turned, after)

    full = [(k, 0) for k in range(ways)]
    pending = None
    ready = []
    for m in sequence[:-1]:
        sent = run(m, 0, window, 0, 1, ready)
        ready = [sent[0]]
        if pending is not None:
            ranked = add(pending[0], 0, window, full, [(g, 0) for g in pending[1]], ranked, ready)
            ready = [sent[0], ranked]
        pending = (m, sent)
    early = run(last, 0, window, 0, 2, ready)
    ranked = add(pending[0], 0, window, full, [(g, 0) for g in pending[1]], ranked, early[:1])
    ready = [early[0], ranked]
    late = []
    for offset in range(0, window, tile):
        late.append(run(last, offset, tile, 1, 2, ready))
        ready = [late[-1][0]]
    slots = full + [(k, half) for k in range(ways)]
    for number, sent in enumerate(late):
        gated = [(g, number) for g in early] + [(g, 0) for g in sent]
        ranked = add(last, number * tile, tile, slots, gated, ranked, ready)
    return ranked


def solution(mesh):
    placed = (
        P(("groups", "req", "rep"), None),
        P(("groups", "req"), "rep"),
        P(("groups", "req"), None),
        P(("groups", "req")),
        P(("groups", "req"), None),
        P(("groups", "req"), None, "head"),
        P(None, "head"),
        P("head", None),
    )

    return jax.shard_map(
        per_device,
        mesh=mesh,
        in_specs=placed,
        out_specs=P(("groups", "req", "rep"), "head"),
        check_vma=False,
    )
```

```python
import math

import jax
import jax.numpy as jnp
from jax import lax
from jax.experimental import pallas as pl
from jax.experimental.pallas import tpu as pltpu
from jax.sharding import PartitionSpec as P

HD = 128
BLOCK = 128
MOSTC = 512
EPSILON = 1e-05
VMEM_LIMIT = 24000 * 1024
PICK_VMEM_LIMIT = 58 * 1024 * 1024


def silu_half(y):
    return y + y * jnp.tanh(y)


def normalize(values):
    center = values - jnp.mean(values, axis=-1, keepdims=True)
    spread = jnp.mean(center * center, axis=-1, keepdims=True)
    return center * lax.rsqrt(spread + EPSILON)


def project_kernel(cand_ref, w_ref, q_ref, g_ref, self_ref):
    heads = q_ref.shape[1] // HD
    scale = 1.0 / math.sqrt(HD)
    normed = normalize(cand_ref[...].astype(jnp.float32)).astype(jnp.bfloat16)
    for h in range(heads):
        part = jnp.dot(
            normed, w_ref[:, h * 4 * HD : (h + 1) * 4 * HD], preferred_element_type=jnp.float32
        )
        part = silu_half(0.5 * part).astype(jnp.bfloat16)
        columns = slice(h * HD, (h + 1) * HD)
        query = part[:, 2 * HD : 3 * HD]
        g_ref[:, columns] = part[:, :HD]
        q_ref[:, columns] = query
        score = jnp.sum(
            query.astype(jnp.float32) * part[:, 3 * HD :].astype(jnp.float32), axis=-1, keepdims=True
        )
        weight = silu_half(score * (0.5 * scale))
        self_ref[:, columns] = weight * part[:, HD : 2 * HD].astype(jnp.float32)


def project(candidates, w_in):
    rows, width = candidates.shape
    columns = w_in.shape[1] // 4
    tile = min(256, rows)
    return pl.pallas_call(
        project_kernel,
        grid=(rows // tile,),
        in_specs=[
            pl.BlockSpec((tile, width), lambda i: (i, 0)),
            pl.BlockSpec(w_in.shape, lambda i: (0, 0), pipeline_mode=pl.Buffered(1)),
        ],
        out_specs=[pl.BlockSpec((tile, columns), lambda i: (i, 0))] * 3,
        out_shape=[
            jax.ShapeDtypeStruct((rows, columns), jnp.bfloat16),
            jax.ShapeDtypeStruct((rows, columns), jnp.bfloat16),
            jax.ShapeDtypeStruct((rows, columns), jnp.float32),
        ],
        cost_estimate=pl.CostEstimate(
            flops=2 * rows * width * 4 * columns,
            bytes_accessed=2 * (rows * width + width * 4 * columns + 4 * rows * columns),
            transcendentals=rows * 4 * columns,
        ),
        compiler_params=pltpu.CompilerParams(vmem_limit_bytes=VMEM_LIMIT),
        name="project",
    )(candidates, w_in)


def window_rows(m, offset, tile):
    def index(i, place, infos):
        first = infos[0, jnp.bitwise_xor(place[0], m)]
        return pl.multiple_of(first + offset + i * tile, 16), 0

    return index


def attend_kernel(m, offset, place, infos, q_ref, g_ref, self_ref, kv_ref, gated_ref):
    tile, width = q_ref.shape
    tokens = kv_ref.shape[1]
    scale = 1.0 / math.sqrt(HD)
    who = jnp.bitwise_xor(place[0], m)
    low = infos[0, who] + offset + pl.program_id(0) * tile
    live = lax.broadcasted_iota(jnp.int32, (1, tokens), 1) < infos[3, who]

    @pl.when(jnp.logical_and(low < infos[2, who], low + tile > infos[1, who]))
    def _():
        for h in range(width // HD):
            cols = slice(h * HD, (h + 1) * HD)
            keys = kv_ref[0, :, 2 * h * HD : (2 * h + 1) * HD]
            values = kv_ref[0, :, (2 * h + 1) * HD : (2 * h + 2) * HD]
            scores = lax.dot_general(
                q_ref[:, cols], keys, (((1,), (1,)), ((), ())), preferred_element_type=jnp.float32
            )
            weights = silu_half(scores * (0.5 * scale))
            weights = jnp.where(live, weights, 0.0).astype(jnp.bfloat16)
            mixed = jnp.dot(weights, values, preferred_element_type=jnp.float32)
            normed = normalize(self_ref[:, cols] + mixed)
            gated_ref[:, cols] = (normed * g_ref[:, cols].astype(jnp.float32)).astype(jnp.bfloat16)


def attend(place, infos, m, offset, size, tile, side, sides, queries, gates, selfs, cached):
    width = queries.shape[1] // sides
    tokens, kvw = cached.shape[1:]
    rows = window_rows(m, offset, tile)
    view = pl.BlockSpec(
        (pl.Element(tile), pl.Element(width)),
        lambda i, place, infos: (rows(i, place, infos)[0], side * width),
    )
    return pl.pallas_call(
        lambda *refs: attend_kernel(m, offset, *refs),
        grid_spec=pltpu.PrefetchScalarGridSpec(
            num_scalar_prefetch=2,
            grid=(size // tile,),
            in_specs=[
                view,
                view,
                view,
                pl.BlockSpec(
                    (1, tokens, kvw), lambda i, place, infos: (0, 0, 0), pipeline_mode=pl.Buffered(1)
                ),
            ],
            out_specs=pl.BlockSpec((tile, width), lambda i, place, infos: (i, 0)),
        ),
        out_shape=jax.ShapeDtypeStruct((size, width), jnp.bfloat16),
        cost_estimate=pl.CostEstimate(
            flops=4 * size * tokens * width,
            bytes_accessed=10 * size * width + 2 * tokens * kvw,
            transcendentals=size * tokens * width // HD,
        ),
        compiler_params=pltpu.CompilerParams(vmem_limit_bytes=VMEM_LIMIT),
        name="attend",
    )(place, infos, queries, gates, selfs, cached)


def finish_kernel(m, offset, slots, place, infos, total_ref, w_ref, *rest):
    gated_refs, out_ref = rest[: len(slots)], rest[-1]
    who = jnp.bitwise_xor(place[0], m)
    tile = total_ref.shape[0]
    low = infos[0, who] + offset + pl.program_id(0) * tile
    position = low + lax.broadcasted_iota(jnp.int32, (tile, 1), 0)
    mine = jnp.logical_and(position >= infos[1, who], position < infos[2, who])
    before = total_ref[...].astype(jnp.float32)
    total = before
    for (k, row), ref in zip(slots, gated_refs):
        total = total + jnp.dot(
            ref[...], w_ref[k, row : row + ref.shape[1], :], preferred_element_type=jnp.float32
        )
    out_ref[...] = jnp.where(mine, total, before).astype(out_ref.dtype)


def finish(place, infos, m, offset, size, tile, slots, gated, total, turned, after=()):
    columns = total.shape[1]
    view = pl.BlockSpec((pl.Element(tile), pl.Element(columns)), window_rows(m, offset, tile))
    blocks = [
        pl.BlockSpec((tile, g.shape[1]), lambda i, place, infos, skip=skip: (i + skip, 0))
        for g, skip in gated
    ]
    arrays = [g for g, _ in gated]
    work = sum(g.shape[1] for g in arrays)
    return pl.pallas_call(
        lambda *refs: finish_kernel(m, offset, slots, *refs),
        grid_spec=pltpu.PrefetchScalarGridSpec(
            num_scalar_prefetch=2,
            grid=(size // tile,),
            in_specs=[
                view,
                pl.BlockSpec(
                    turned.shape, lambda i, place, infos: (0, 0, 0), pipeline_mode=pl.Buffered(1)
                ),
            ]
            + blocks
            + [pl.BlockSpec(memory_space=pl.ANY)] * len(after),
            out_specs=view,
        ),
        out_shape=jax.ShapeDtypeStruct(total.shape, total.dtype),
        input_output_aliases={2: 0},
        cost_estimate=pl.CostEstimate(
            flops=2 * size * columns * work,
            bytes_accessed=4 * size * columns + 2 * size * work + 2 * work * columns,
            transcendentals=0,
        ),
        compiler_params=pltpu.CompilerParams(vmem_limit_bytes=VMEM_LIMIT),
        name="finish",
    )(place, infos, total, turned, *arrays, *after)


def pick_kernel(place, table, kv_ref, *rest):
    rest[-1][...] = kv_ref[...]


def pick(place, table, count, kv_cache, m, side, sides, after):
    user = lambda i, place, table: (table[jnp.bitwise_xor(place[0], m) * count + place[0]], i, side)
    tokens, kvw = kv_cache.shape[1], kv_cache.shape[2] // sides
    block = (1, tokens, kvw)
    return pl.pallas_call(
        pick_kernel,
        grid_spec=pltpu.PrefetchScalarGridSpec(
            num_scalar_prefetch=2,
            grid=(1,),
            in_specs=[pl.BlockSpec(block, user)] + [pl.BlockSpec(memory_space=pl.ANY)] * len(after),
            out_specs=pl.BlockSpec(block, lambda i, place, table: (0, i, 0)),
        ),
        out_shape=jax.ShapeDtypeStruct((1, tokens, kvw), kv_cache.dtype),
        compiler_params=pltpu.CompilerParams(vmem_limit_bytes=PICK_VMEM_LIMIT),
        name="pick",
    )(place, table, kv_cache, *after)


def exchange_order(count):
    far = [m for m in range(count) if 2 * m >= count][::-1]
    near = [m for m in range(2, count) if 2 * m < count][::-1]
    order = []
    while far or near:
        order += far[:1] + (near[:1] if len(far) > 2 or not far else [])
        near = near[1:] if len(far) > 2 or not far else near
        far = far[1:]
    return order


def per_device(
    candidates,
    candidate_request,
    request_owner,
    request_user,
    request_blocks,
    kv_cache,
    w_in,
    w_out,
):
    rows, width = candidates.shape
    count = lax.axis_size("req")
    ways = lax.axis_size("head")
    myself = lax.axis_index("req")
    side = lax.axis_index("head")
    columns = width // ways
    window = min(MOSTC + 16, rows)
    owners = request_owner[:, 0]
    everyone = jnp.arange(count, dtype=jnp.int32)
    names = (owners[None, :] == everyone[:, None]).astype(jnp.int32)
    wanted = jnp.sum(names * request_user[None, :], axis=1)
    spread = jnp.where(everyone[:, None] == myself, wanted[None, :], 0)
    table = lax.psum(spread.reshape(-1), "req")
    place = myself[None].astype(jnp.int32)

    order = exchange_order(count)
    arrived = {}
    after = []
    last = order[-1]
    for m in order + [1, 0]:
        sides = 2 if m == last else 1
        arrived[m] = []
        for part in range(sides):
            picked = pick(place, table, count, kv_cache, m, part, sides, after)
            after = [picked]
            if m:
                picked = lax.ppermute(picked, "req", [(i, i ^ m) for i in range(count)])
            arrived[m].append(picked)

    segment = candidate_request[0]
    served = jnp.sum(names * jnp.arange(owners.shape[0], dtype=jnp.int32)[None, :], axis=1)
    starts = jnp.sum((segment[None, :] < served[:, None]).astype(jnp.int32), axis=1)
    ends = jnp.sum((segment[None, :] <= served[:, None]).astype(jnp.int32), axis=1)
    exists = jnp.sum(names, axis=1) > 0
    ends = jnp.where(exists, ends, starts)
    live = jnp.sum(names * request_blocks[0][None, :], axis=1) * BLOCK
    firsts = jnp.minimum(starts // 16 * 16, rows - window)
    infos = jnp.stack([firsts, starts, ends, live])

    queries, gates, selfs = project(candidates, w_in)

    def to_peer(value, k):
        return lax.ppermute(value, "head", [(i, (i + k) % ways) for i in range(ways)])

    w_out, _ = lax.optimization_barrier((w_out, after[0]))
    turned = []
    for k in range(ways):
        piece = lax.dynamic_slice_in_dim(w_out, ((side + k) % ways) * columns, columns, 1)
        turned.append(to_peer(piece, k) if k else piece)
    turned = jnp.stack(turned)
    ranked = lax.dynamic_slice_in_dim(candidates, side * columns, columns, 1)
    sequence = [0, 1] + order
    tile = window // 3 if window % 48 == 0 else window
    half = w_out.shape[0] // 2

    def run(m, offset, size, part, sides, ready):
        current = infos
        if ready:
            current, *ready = lax.optimization_barrier((infos, *ready))
        gated = attend(
            place, current, m, offset, size, tile, part, sides, queries, gates, selfs, arrived[m][part]
        )
        return [gated] + [to_peer(gated, k) for k in range(1, ways)]

    def add(m, offset, size, slots, gated, ranked, after):
        return finish(place, infos, m, offset, size, tile, slots, gated, ranked, turned, after)

    full = [(k, 0) for k in range(ways)]
    pending = None
    ready = []
    for m in sequence[:-1]:
        sent = run(m, 0, window, 0, 1, ready)
        ready = [sent[0]]
        if pending is not None:
            ranked = add(pending[0], 0, window, full, [(g, 0) for g in pending[1]], ranked, ready)
            ready = [sent[0], ranked]
        pending = (m, sent)
    early = run(last, 0, window, 0, 2, ready)
    ranked = add(pending[0], 0, window, full, [(g, 0) for g in pending[1]], ranked, early[:1])
    ready = [early[0], ranked]
    late = []
    for offset in range(0, window, tile):
        late.append(run(last, offset, tile, 1, 2, ready))
        ready = [late[-1][0]]
    slots = full + [(k, half) for k in range(ways)]
    for number, sent in enumerate(late):
        gated = [(g, number) for g in early] + [(g, 0) for g in sent]
        ranked = add(last, number * tile, tile, slots, gated, ranked, ready)
    return ranked


def solution(mesh):
    placed = (
        P(("groups", "req", "rep"), None),
        P(("groups", "req"), "rep"),
        P(("groups", "req"), None),
        P(("groups", "req")),
        P(("groups", "req"), None),
        P(("groups", "req"), None, "head"),
        P(None, "head"),
        P("head", None),
    )

    return jax.shard_map(
        per_device,
        mesh=mesh,
        in_specs=placed,
        out_specs=P(("groups", "req", "rep"), "head"),
        check_vma=False,
    )
```
